32 devices in a mesh: seq: 16 (over z, x, core), head: 2 (over y).
Axes of the slice: x: 2, y: 2, z: 4, core: 2. Of those that a mesh axis runs over, the one named last changes fastest.
Arguments:
- queries: bfloat16 [2048, 2048], P('seq', 'head'), may hold values from -5 to 5
- keys: bfloat16 [2048, 2048], P('seq', 'head'), may hold values from -5 to 5
- values: bfloat16 [2048, 2048], P('seq', 'head'), may hold values from -6 to 6
- grad_out: bfloat16 [2048, 2048], P('seq', 'head'), may hold values from -6 to 6
- doc_ids: int32 [2048], P(('seq', 'head')), may hold values from 0 to 31, never falling along the last dimension, each value on 1 to 512 neighbouring positions
- loss_mask: int32 [2048], P(('seq', 'head')), may hold values 0 or 1
Outputs:
- attended: bfloat16 [2048, 2048], P('seq', 'head')
- query_grad: bfloat16 [2048, 2048], P('seq', 'head')
- key_grad: bfloat16 [2048, 2048], P('seq', 'head')
- value_grad: bfloat16 [2048, 2048], P('seq', 'head')
The draws below stay inside these ranges and needn't reach their ends.
Inputs may be any that keep to these rules, and one draw needn't show every extreme that they name: `doc_ids`: documents are runs of consecutive tokens numbered 0, 1, 2, ... in order; each has 1 to 512 tokens.
All inputs are finite; a program needn't handle non-finite values. No bound on the sum of `loss_mask` on one device may be relied on, other than what follows from the above.
Results may differ from the reference program's by a relative error of at most 0.033.
Values may be sent and summed in bfloat16 or wider, within the bound.
No kernel may reach another device: no remote copies, remote signals or barrier semaphores. Data moves between devices by JAX's collectives and lax.ppermute only.
A program may use at most 64 MiB of HBM per device.

```python
import math
import jax
import jax.numpy as jnp
import numpy as np
from jax import lax

TOK_DEV = 128
HEAD_DIM = 128
HEADS = 16
WINDOW = 512
TOKENS = 2048
DOCS = 32
MOST_DOC = 512
N_SEQ = 16


def shared_pair(key):
    width = HEADS * HEAD_DIM
    key_query = jax.random.fold_in(key, 101)
    key_key = jax.random.fold_in(key, 102)
    query_rows = jnp.clip(jax.random.normal(key_query, (TOKENS, width), jnp.float32), -5.0, 5.0)
    key_rows = jnp.clip(jax.random.normal(key_key, (TOKENS, width), jnp.float32), -5.0, 5.0)
    return (query_rows.astype(jnp.bfloat16), key_rows.astype(jnp.bfloat16))


def draw_queries(key, part):
    return shared_pair(key)[0]


def draw_keys(key, part):
    return shared_pair(key)[1]


def set_ends(drawn, stream_key, low, high):
    longest = drawn.shape.index(max(drawn.shape))
    spots = []
    for shift in (0, 1):
        where = [jax.random.randint(jax.random.fold_in(stream_key, axis), (), 0, length) for axis, length in enumerate(drawn.shape)]
        where[longest] = (where[longest] + shift) % drawn.shape[longest]
        spots.append(tuple(where))
    return drawn.at[spots[0]].set(low).at[spots[1]].set(high)


def level_of(rng, dims, pieces, low, largest):
    def one(position, parts):
        heights = jax.random.uniform(jax.random.fold_in(jax.random.fold_in(rng, 6), position), (parts,), jnp.float32, low / len(pieces), largest / len(pieces))
        return jnp.repeat(jnp.exp(heights), dims[position] // parts).reshape((-1,) + (1,) * (len(dims) - position - 1))

    loudness = one(*pieces[0])
    for cut in pieces[1:]:
        loudness = loudness * one(*cut)
    return loudness


def profile(number_of, total, reach, skew):
    loads = [(1 << 20) // math.isqrt(standing ** skew) + 1 for standing in range(2, number_of + 1)]
    spare, given = total - reach - (number_of - 1), [1] * (number_of - 1)
    while spare > 0:
        free = [i for i in range(number_of - 1) if given[i] < reach]
        whole, budget = sum([loads[i] for i in free]), spare
        for i in free:
            addition = min(reach - given[i], max(1, budget * loads[i] // whole), spare)
            given[i] = given[i] + addition
            spare = spare - addition
    return np.array([reach] + given)


def uneven_parts(stream_key, amount, total, reach, lean):
    if amount == 2:
        one = jax.random.randint(stream_key, (), max(1, total - reach), min(reach, total - 1) + 1)
        return jnp.stack([one, total - one])
    tallies = jnp.asarray(profile(amount, total, reach, lean), jnp.int32)
    pairs = (amount - 1) // 2
    giver, sink = tallies[1:1 + 2 * pairs:2], tallies[2:2 + 2 * pairs:2]
    slack = jnp.minimum(giver - 1, reach - sink)
    passed = jax.random.randint(jax.random.fold_in(stream_key, 1), (pairs,), 0, 1 << 20) % (slack + 1)
    tallies = tallies.at[1:1 + 2 * pairs:2].set(giver - passed).at[2:2 + 2 * pairs:2].set(sink + passed)
    return tallies[jax.random.permutation(jax.random.fold_in(stream_key, 2), amount)]


def gaussian(rng, shape, deviation, reach, shards=(), kind=jnp.bfloat16):
    drawn = jax.random.normal(rng, shape, jnp.float32) * deviation
    if len(shards) > 0:
        drawn = level_of(rng, shape, shards, -0.22, 0.18) * drawn
    return jnp.clip(drawn, min=-reach, max=reach).astype(kind)


def setup_inputs(seed: int = 0) -> dict:
    seeds = jax.random.split(jax.random.key(seed), 7)
    return {
        "queries": draw_queries(jax.random.fold_in(seeds[6], 71), 0),
        "keys": draw_keys(jax.random.fold_in(seeds[6], 71), 0),
        "values": gaussian(seeds[2], (TOKENS, HEADS * HEAD_DIM), 1.0, 6.0, ((0, 16), (1, 2))),
        "grad_out": gaussian(seeds[3], (TOKENS, HEADS * HEAD_DIM), 1.0, 6.0, ((0, 16), (1, 2))),
        "doc_ids": jnp.searchsorted(jnp.cumsum(uneven_parts(seeds[4], DOCS, TOKENS, MOST_DOC, 2)), jnp.arange(TOKENS), side="right").astype(jnp.int32),
        "loss_mask": set_ends((jax.random.randint(seeds[5], (TOKENS,), 0, 4) < 3).astype(jnp.int32), jax.random.fold_in(seeds[5], 1), 0, 1),
    }


masked_value = -1e+30

def rounded(values_in):
    return lax.optimization_barrier(values_in.astype(jnp.bfloat16)).astype(jnp.float32)

def by_head(rows):
    return rows.astype(jnp.float32).reshape(rows.shape[0], -1, HEAD_DIM)

def masked_scores(q_rows, k_rows, q_pos, k_pos, q_start):
    score = jnp.einsum('qhd,khd->hqk', by_head(q_rows), by_head(k_rows)) * (1.0 / math.sqrt(HEAD_DIM))
    later = k_pos[None, :] <= q_pos[:, None]
    inside = k_pos[None, :] > q_pos[:, None] - WINDOW
    same_doc = k_pos[None, :] >= q_start[:, None]
    return jnp.where((later & inside & same_doc)[None], score, masked_value)

def reference(queries, keys, values, grad_out, doc_ids, loss_mask):
    width = queries.shape[1]
    head_count = width // HEAD_DIM
    scaling = 1.0 / math.sqrt(HEAD_DIM)
    positions = jnp.arange(TOKENS, dtype=jnp.int32)
    change = jnp.concatenate([jnp.ones((1,), dtype=bool), doc_ids[1:] != doc_ids[:-1]])
    doc_start = lax.cummax(jnp.where(change, positions, 0), axis=0).astype(jnp.int32)
    counts = jax.ops.segment_sum(loss_mask.astype(jnp.float32), doc_ids, num_segments=DOCS)
    weight = loss_mask.astype(jnp.float32) * TOK_DEV / jnp.maximum(counts[doc_ids], TOK_DEV // 8)
    padding = jnp.zeros((WINDOW, width), queries.dtype)
    keys_left = jnp.concatenate([padding, keys])
    values_left = jnp.concatenate([padding, values])
    block_ids = jnp.arange(N_SEQ, dtype=jnp.int32)

    def forward(block_id):
        first_row = block_id * TOK_DEV
        q_rows = lax.dynamic_slice_in_dim(queries, first_row, TOK_DEV, 0)
        k_rows = lax.dynamic_slice_in_dim(keys_left, first_row, TOK_DEV + WINDOW, 0)
        v_rows = lax.dynamic_slice_in_dim(values_left, first_row, TOK_DEV + WINDOW, 0)
        q_pos = first_row + jnp.arange(TOK_DEV, dtype=jnp.int32)
        k_pos = first_row - WINDOW + jnp.arange(TOK_DEV + WINDOW, dtype=jnp.int32)
        q_start = lax.dynamic_slice_in_dim(doc_start, first_row, TOK_DEV, 0)
        score = masked_scores(q_rows, k_rows, q_pos, k_pos, q_start)
        row_max = lax.optimization_barrier(jnp.max(score, axis=2))
        log_block = row_max + jnp.log(lax.optimization_barrier(jnp.sum(jnp.exp(score - row_max[..., None]), axis=2)))
        prob = jnp.exp(score - log_block[..., None])
        mixed = jnp.einsum('hqk,khd->qhd', rounded(prob), by_head(v_rows))
        return (mixed.reshape(TOK_DEV, width).astype(jnp.bfloat16), log_block)
    out_blocks, log_blocks = lax.map(forward, block_ids)
    attended = lax.optimization_barrier(out_blocks.reshape(TOKENS, width))
    log_total = jnp.transpose(log_blocks, (1, 0, 2)).reshape(head_count, TOKENS)
    grad_rows = lax.optimization_barrier((weight[:, None] * grad_out.astype(jnp.float32)).astype(jnp.bfloat16))
    row_delta = lax.optimization_barrier(jnp.sum(by_head(grad_rows) * by_head(attended), axis=2)).T

    def query_side(block_id):
        first_row = block_id * TOK_DEV
        q_rows = lax.dynamic_slice_in_dim(queries, first_row, TOK_DEV, 0)
        g_rows = lax.dynamic_slice_in_dim(grad_rows, first_row, TOK_DEV, 0)
        k_rows = lax.dynamic_slice_in_dim(keys_left, first_row, TOK_DEV + WINDOW, 0)
        v_rows = lax.dynamic_slice_in_dim(values_left, first_row, TOK_DEV + WINDOW, 0)
        q_pos = first_row + jnp.arange(TOK_DEV, dtype=jnp.int32)
        k_pos = first_row - WINDOW + jnp.arange(TOK_DEV + WINDOW, dtype=jnp.int32)
        q_start = lax.dynamic_slice_in_dim(doc_start, first_row, TOK_DEV, 0)
        log_block = lax.dynamic_slice_in_dim(log_total, first_row, TOK_DEV, 1)
        delta_block = lax.dynamic_slice_in_dim(row_delta, first_row, TOK_DEV, 1)
        score = masked_scores(q_rows, k_rows, q_pos, k_pos, q_start)
        prob = jnp.exp(score - log_block[..., None])
        prob_grad = jnp.einsum('qhd,khd->hqk', by_head(g_rows), by_head(v_rows))
        score_grad = rounded(prob * (prob_grad - delta_block[..., None]) * scaling)
        result = jnp.einsum('hqk,khd->qhd', score_grad, by_head(k_rows))
        return result.reshape(TOK_DEV, width).astype(jnp.bfloat16)
    query_grad = lax.map(query_side, block_ids).reshape(TOKENS, width)
    q_right = jnp.concatenate([queries, padding])
    g_right = jnp.concatenate([grad_rows, padding.astype(grad_rows.dtype)])
    log_right = jnp.concatenate([log_total, jnp.zeros((head_count, WINDOW), jnp.float32)], axis=1)
    delta_right = jnp.concatenate([row_delta, jnp.zeros((head_count, WINDOW), jnp.float32)], axis=1)
    start_right = jnp.concatenate([doc_start, jnp.full((WINDOW,), TOKENS, jnp.int32)])

    def key_side(block_id):
        first_row = block_id * TOK_DEV
        k_rows = lax.dynamic_slice_in_dim(keys, first_row, TOK_DEV, 0)
        v_rows = lax.dynamic_slice_in_dim(values, first_row, TOK_DEV, 0)
        q_rows = lax.dynamic_slice_in_dim(q_right, first_row, TOK_DEV + WINDOW, 0)
        g_rows = lax.dynamic_slice_in_dim(g_right, first_row, TOK_DEV + WINDOW, 0)
        log_block = lax.dynamic_slice_in_dim(log_right, first_row, TOK_DEV + WINDOW, 1)
        delta_block = lax.dynamic_slice_in_dim(delta_right, first_row, TOK_DEV + WINDOW, 1)
        q_start = lax.dynamic_slice_in_dim(start_right, first_row, TOK_DEV + WINDOW, 0)
        q_pos = first_row + jnp.arange(TOK_DEV + WINDOW, dtype=jnp.int32)
        k_pos = first_row + jnp.arange(TOK_DEV, dtype=jnp.int32)
        score = masked_scores(q_rows, k_rows, q_pos, k_pos, q_start)
        prob = jnp.exp(score - log_block[..., None])
        prob_grad = jnp.einsum('qhd,khd->hqk', by_head(g_rows), by_head(v_rows))
        score_grad = rounded(prob * (prob_grad - delta_block[..., None]) * scaling)
        key_part = jnp.einsum('hqk,qhd->khd', score_grad, by_head(q_rows))
        value_part = jnp.einsum('hqk,qhd->khd', rounded(prob), by_head(g_rows))
        return (key_part.reshape(TOK_DEV, width).astype(jnp.bfloat16), value_part.reshape(TOK_DEV, width).astype(jnp.bfloat16))
    key_blocks, value_blocks = lax.map(key_side, block_ids)
    return (attended, query_grad, key_blocks.reshape(TOKENS, width), value_blocks.reshape(TOKENS, width))
```

```python
import functools
import math

import jax
import jax.numpy as jnp
from jax import lax
from jax.experimental import pallas as pl
from jax.experimental.pallas import tpu as pltpu
from jax.sharding import PartitionSpec as P


HEAD_DIM = 128
WINDOW = 512
MASKED = -1e30
META_ROWS = 16


bf16, f32 = jnp.bfloat16, jnp.float32
VMEM = pl.BlockSpec(memory_space=pltpu.VMEM)


def dot_nt(a, b):
    return lax.dot_general(a, b, (((1,), (1,)), ((), ())), preferred_element_type=f32)


def dot_nn(a, b):
    return lax.dot_general(a, b, (((1,), (0,)), ((), ())), preferred_element_type=f32)


def route_x(n, cross):
    return [(i, i ^ (3 if cross else 2)) for i in range(n)]


def route_diag(n, cross):
    route = []
    for i in range(n):
        j = i + 2 if (i >> 1) & 1 else i - 2
        route.append((i, j ^ cross if 0 <= j < n else i ^ 1))
    return route


def route_even(n, cross):
    return [(i, i ^ (5 if cross else 4)) for i in range(n)]


def route_odd(n, cross):
    route = []
    for i in range(n):
        j = i + 4 if (i >> 2) & 1 else i - 4
        route.append((i, j ^ cross if 0 <= j < n else i ^ 1))
    return route


def place():
    index = lax.axis_index("seq")
    core = lax.rem(index, 2)
    pair = lax.rem(lax.div(index, 2), 2)
    plane_odd = lax.rem(lax.div(index, 4), 2)
    return index, core, pair, plane_odd


def prep_kernel(heads, q, k, v, g, mark, x1, x2, a1, a2, b1, b2, d1, d2, cc):
    _, core, pair, plane_odd = place()
    rows = q.shape[0]
    mark_v = mark[...]
    high = jnp.floor(mark_v * (1.0 / 256.0))
    low = mark_v - high * 256.0
    row = lax.broadcasted_iota(jnp.int32, (META_ROWS, rows), 0)
    meta = jnp.where(row == 0, high, jnp.where(row == 1, low, 0.0)).astype(bf16)
    for ref in (x1, x2, a1, a2, b1, b2, d1, d2):
        ref[2 * heads * rows :, :] = meta
    cc[4 * heads * rows :, :] = meta

    def tile(ref, group, h):
        start = pl.multiple_of((group * heads + h) * HEAD_DIM, HEAD_DIM)
        return ref[:, pl.ds(start, HEAD_DIM)]

    def fill(first, second, group, refs):
        for h in range(heads):
            one, two = tile(first, group, h), tile(second, group, h)
            for ref in refs:
                ref[h * rows : (h + 1) * rows, :] = one
                ref[(heads + h) * rows : (heads + h + 1) * rows, :] = two

    for group, xs, ds, as_, bs in ((core, x1, d1, a1, b1), (1 - core, x2, d2, a2, b2)):

        @pl.when((pair == 0) & (plane_odd == 0))
        def _():
            fill(k, v, group, (xs, as_))
            fill(q, g, group, (ds, bs))

        @pl.when((pair == 0) & (plane_odd == 1))
        def _():
            fill(k, v, group, (xs, bs))
            fill(q, g, group, (ds, as_))

        @pl.when((pair == 1) & (plane_odd == 0))
        def _():
            fill(k, v, group, (ds, as_))
            fill(q, g, group, (xs, bs))

        @pl.when((pair == 1) & (plane_odd == 1))
        def _():
            fill(k, v, group, (ds, bs))
            fill(q, g, group, (xs, as_))

    for n, ref in enumerate((q, g, k, v)):
        for h in range(heads):
            at = (n * heads + h) * rows
            cc[at : at + rows, :] = tile(ref, 1 - core, h)


def marks_of(meta):
    value = meta[0:1, :] * 256.0 + meta[1:2, :]
    doc = jnp.floor(value * 0.5)
    return doc, value - 2.0 * doc


def read_marks(ref, at):
    return marks_of(ref[at : at + META_ROWS, :].astype(f32))


def column_of(row):
    return jnp.transpose(jnp.broadcast_to(row, (HEAD_DIM, row.shape[1])))


def own_marks(mark, cc, heads, rows):
    value = mark[...]
    doc = jnp.floor(value * 0.5)
    other_doc, other_loss = read_marks(cc, 4 * heads * rows)
    return [(doc, value - 2.0 * doc), (other_doc, other_loss)]


def chip_positions(core, rows, axis, shape):
    spot = lax.broadcasted_iota(jnp.int32, shape, axis)
    return spot + jnp.where(spot < rows, core * rows, -core * rows)


def query_kernel(
    heads, chips, q, k, v, g, mark, cc, x1, x2, a1, a2, b1, b2, d1, d2,
    att_own, dq_own, send, stats, bias,
):
    index, core, pair, plane_odd = place()
    chip = lax.div(index, 2)
    rows = q.shape[0]
    scale = 1.0 / math.sqrt(HEAD_DIM)
    is_one, is_odd = pair == 1, plane_odd == 1
    meta_at = 2 * heads * rows

    def either(flag, one, two):
        return jnp.where(flag, one, two)

    def marks(flag, one, two, valid):
        doc_a, loss_a = read_marks(one, meta_at)
        doc_b, loss_b = read_marks(two, meta_at)
        doc = either(flag, doc_a, doc_b)
        return jnp.where(valid, doc, -1.0), either(flag, loss_a, loss_b)

    own = own_marks(mark, cc, heads, rows)
    left_1, left_2 = chip >= 1, chip >= 2
    right_1, right_2 = chip < chips - 1, chip < chips - 2
    m1 = [marks(is_one, x1, d1, left_1), marks(is_one, x2, d2, left_1)]
    m2 = [marks(is_odd, a1, b1, left_2), marks(is_odd, a2, b2, left_2)]
    p1 = [marks(is_one, d1, x1, right_1), marks(is_one, d2, x2, right_1)]
    p2 = [marks(is_odd, b1, a1, right_2), marks(is_odd, b2, a2, right_2)]

    q_doc = column_of(jnp.concatenate([own[0][0], own[1][0]], axis=1))
    q_loss = column_of(jnp.concatenate([own[0][1], own[1][1]], axis=1))
    total = jnp.zeros((2 * rows, HEAD_DIM), f32)
    for doc, loss in own + m1 + m2 + p1 + p2:
        total = total + jnp.where(q_doc == doc, loss, 0.0)
    count = jnp.sum(total, axis=1, keepdims=True)
    weight = q_loss[:, 0:1] * (float(rows) / jnp.maximum(count, float(rows // 8)))

    q_pos = chip_positions(core, rows, 0, (2 * rows, HEAD_DIM))
    spot = lax.broadcasted_iota(jnp.int32, (2 * rows, HEAD_DIM), 1)
    offsets = [core * rows, (1 - core) * rows]
    offsets = offsets + [o - 2 * rows for o in offsets] + [o - 4 * rows for o in offsets]
    for n, (doc, _) in enumerate(own + m1 + m2):
        gap = q_pos - (spot + offsets[n])
        fine = (gap >= 0) & (gap < WINDOW) & (q_doc == doc)
        bias[:, n * rows : (n + 1) * rows] = jnp.where(fine, 0.0, MASKED)

    lane = lax.broadcasted_iota(jnp.int32, (2 * rows, HEAD_DIM), 1)
    table = jnp.where(lane == 2 * heads, weight, 0.0)

    def local(ref, n, h):
        start = pl.multiple_of((core * heads + h) * HEAD_DIM, HEAD_DIM)
        at = (n * heads + h) * rows
        return [ref[:, pl.ds(start, HEAD_DIM)], cc[at : at + rows, :]]

    def halo(n, h):
        at = pl.ds((n * heads + h) * rows, rows)
        return [
            either(is_one, x1[at, :], d1[at, :]),
            either(is_one, x2[at, :], d2[at, :]),
            either(is_odd, a1[at, :], b1[at, :]),
            either(is_odd, a2[at, :], b2[at, :]),
        ]

    for h in range(heads):
        q_rows = jnp.concatenate(local(q, 0, h), axis=0)
        g_rows = jnp.concatenate(local(g, 1, h), axis=0)
        k_rows = jnp.concatenate(local(k, 2, h) + halo(0, h), axis=0)
        v_rows = jnp.concatenate(local(v, 3, h) + halo(1, h), axis=0)
        score = dot_nt(q_rows, k_rows) * scale + bias[...]
        top = jnp.max(score, axis=1, keepdims=True)
        prob = jnp.exp(score - top)
        norm = jnp.sum(prob, axis=1, keepdims=True)
        share = 1.0 / norm
        att = (dot_nn(prob.astype(bf16), v_rows) * share).astype(bf16)
        delta = jnp.sum(g_rows.astype(f32) * att.astype(f32), axis=1, keepdims=True)
        slope = (prob * (dot_nt(g_rows, v_rows) - delta)).astype(bf16)
        dq = (dot_nn(slope, k_rows) * (share * weight * scale)).astype(bf16)
        att_own[:, h * HEAD_DIM : (h + 1) * HEAD_DIM] = att[:rows]
        dq_own[:, h * HEAD_DIM : (h + 1) * HEAD_DIM] = dq[:rows]
        send[h * rows : (h + 1) * rows, :] = att[rows:]
        send[(heads + h) * rows : (heads + h + 1) * rows, :] = dq[rows:]
        table = jnp.where(lane == h, top + jnp.log(norm), table)
        table = jnp.where(lane == heads + h, delta, table)
    stats[...] = jnp.transpose(table)[:META_ROWS, :]


def key_kernel(
    heads, chips, q, k, v, g, mark, cc, x1, x2, a1, a2, b1, b2, d1, d2, stats, stats_1, stats_2,
    dk_own, dv_own, send, bias,
):
    index, core, pair, plane_odd = place()
    chip = lax.div(index, 2)
    rows = q.shape[0]
    scale = 1.0 / math.sqrt(HEAD_DIM)
    is_one, is_odd = pair == 1, plane_odd == 1
    meta_at = 2 * heads * rows

    def either(flag, one, two):
        return jnp.where(flag, one, two)

    def doc_row(flag, one, two, valid):
        doc = either(flag, read_marks(one, meta_at)[0], read_marks(two, meta_at)[0])
        return jnp.where(valid, doc, -1.0)

    own = [m[0] for m in own_marks(mark, cc, heads, rows)]
    right_1, right_2 = chip < chips - 1, chip < chips - 2
    p1 = [doc_row(is_one, d1, x1, right_1), doc_row(is_one, d2, x2, right_1)]
    p2 = [doc_row(is_odd, b1, a1, right_2), doc_row(is_odd, b2, a2, right_2)]
    k_doc = column_of(jnp.concatenate(own, axis=1))
    k_pos = chip_positions(core, rows, 0, (2 * rows, HEAD_DIM))
    spot = lax.broadcasted_iota(jnp.int32, (2 * rows, HEAD_DIM), 1)
    offsets = [core * rows, (1 - core) * rows]
    offsets = offsets + [o + 2 * rows for o in offsets] + [o + 4 * rows for o in offsets]
    for n, doc in enumerate(own + p1 + p2):
        gap = spot + offsets[n] - k_pos
        fine = (gap >= 0) & (gap < WINDOW) & (k_doc == doc)
        bias[:, n * rows : (n + 1) * rows] = jnp.where(fine, 0.0, MASKED)

    def local(ref, n, h):
        start = pl.multiple_of((core * heads + h) * HEAD_DIM, HEAD_DIM)
        at = (n * heads + h) * rows
        return [ref[:, pl.ds(start, HEAD_DIM)], cc[at : at + rows, :]]

    def halo(n, h):
        at = pl.ds((n * heads + h) * rows, rows)
        return [
            either(is_one, d1[at, :], x1[at, :]),
            either(is_one, d2[at, :], x2[at, :]),
            either(is_odd, b1[at, :], a1[at, :]),
            either(is_odd, b2[at, :], a2[at, :]),
        ]

    def line(n):
        return jnp.concatenate([s[n : n + 1, :] for s in (stats, stats_1, stats_2)], axis=1)

    weight = line(2 * heads)
    for h in range(heads):
        k_rows = jnp.concatenate(local(k, 2, h), axis=0)
        v_rows = jnp.concatenate(local(v, 3, h), axis=0)
        q_rows = jnp.concatenate(local(q, 0, h) + halo(0, h), axis=0)
        g_rows = jnp.concatenate(local(g, 1, h) + halo(1, h), axis=0)
        score = dot_nt(k_rows, q_rows) * scale + bias[...]
        prob = jnp.exp(score - line(h)) * weight
        slope = (prob * (dot_nt(v_rows, g_rows) - line(heads + h))).astype(bf16)
        dv = dot_nn(prob.astype(bf16), g_rows).astype(bf16)
        dk = (dot_nn(slope, q_rows) * scale).astype(bf16)
        dk_own[:, h * HEAD_DIM : (h + 1) * HEAD_DIM] = dk[:rows]
        dv_own[:, h * HEAD_DIM : (h + 1) * HEAD_DIM] = dv[:rows]
        send[h * rows : (h + 1) * rows, :] = dk[rows:]
        send[(heads + h) * rows : (heads + h + 1) * rows, :] = dv[rows:]


def join_kernel(heads, one, two, got, out_one, out_two):
    _, core, _, _ = place()
    rows, half = one.shape
    here = pl.multiple_of(core * half, HEAD_DIM)
    out_one[:, pl.ds(here, half)] = one[...]
    out_two[:, pl.ds(here, half)] = two[...]
    for n, out in enumerate((out_one, out_two)):
        for h in range(heads):
            at = (n * heads + h) * rows
            start = pl.multiple_of((1 - core) * half + h * HEAD_DIM, HEAD_DIM)
            out[:, pl.ds(start, HEAD_DIM)] = got[at : at + rows, :]


def run(kernel, outs, args, scratch=(), flops=0):
    size = sum(math.prod(a.shape) * a.dtype.itemsize for a in args)
    size = size + sum(math.prod(o.shape) * o.dtype.itemsize for o in outs)
    return pl.pallas_call(
        kernel,
        out_shape=outs,
        in_specs=[VMEM] * len(args),
        out_specs=[VMEM] * len(outs),
        scratch_shapes=list(scratch),
        cost_estimate=pl.CostEstimate(flops=flops, bytes_accessed=size, transcendentals=0),
    )(*args)


def body(queries, keys, values, grad_out, doc_ids, loss_mask):
    rows, width = queries.shape
    heads = width // HEAD_DIM // 2
    half = heads * HEAD_DIM
    n = lax.axis_size("seq")
    chips = n // 2
    shape = jax.ShapeDtypeStruct

    def move(value, route, axis="seq"):
        return lax.ppermute(value, axis, route)

    mine = (doc_ids * 2 + loss_mask).astype(f32)
    theirs = move(mine, [(0, 1), (1, 0)], "head")
    first = lax.axis_index("head") == 0
    mark = jnp.concatenate([jnp.where(first, mine, theirs), jnp.where(first, theirs, mine)])
    mark = mark[None, :]

    bundle = shape((2 * heads * rows + META_ROWS, HEAD_DIM), bf16)
    double = shape((4 * heads * rows + META_ROWS, HEAD_DIM), bf16)
    packs = run(
        functools.partial(prep_kernel, heads),
        [bundle] * 8 + [double],
        (queries, keys, values, grad_out, mark),
    )
    x1, x2, a1, a2, b1, b2, d1, d2, cc = packs
    x1 = move(x1, route_x(n, 0))
    a1 = move(a1, route_even(n, 0))
    b1 = move(b1, route_odd(n, 0))
    d1 = move(d1, route_diag(n, 0))
    x2 = move(x2, route_x(n, 1))
    a2 = move(a2, route_even(n, 1))
    b2 = move(b2, route_odd(n, 1))
    d2 = move(d2, route_diag(n, 1))
    cc = move(cc, [(i, i ^ 1) for i in range(n)])

    common = (queries, keys, values, grad_out, mark, cc, x1, x2, a1, a2, b1, b2, d1, d2)
    side = shape((rows, half), bf16)
    pack = shape((2 * heads * rows, HEAD_DIM), bf16)
    table = shape((META_ROWS, 2 * rows), f32)
    bias = pltpu.VMEM((2 * rows, 6 * rows), f32)
    flops = 4 * heads * 2 * (2 * rows) * (6 * rows) * HEAD_DIM
    att, dq, send_1, stats = run(
        functools.partial(query_kernel, heads, chips),
        [side, side, pack, table],
        common,
        [bias],
        flops,
    )
    stats_1 = move(stats, [(i, (i - 2) % n) for i in range(n)])
    stats_2 = move(stats, [(i, (i - 4) % n) for i in range(n)])
    got_1 = move(send_1, [(i, i ^ 1) for i in range(n)])
    dk, dv, send_2 = run(
        functools.partial(key_kernel, heads, chips),
        [side, side, pack],
        common + (stats, stats_1, stats_2),
        [bias],
        flops,
    )
    got_2 = move(send_2, [(i, i ^ 1) for i in range(n)])
    whole = shape((rows, width), bf16)
    join = functools.partial(join_kernel, heads)
    attended, query_grad = run(join, [whole, whole], (att, dq, got_1))
    key_grad, value_grad = run(join, [whole, whole], (dk, dv, got_2))
    return attended, query_grad, key_grad, value_grad


def solution(mesh):
    wide = P("seq", "head")
    flat = P(("seq", "head"))
    return jax.shard_map(
        body,
        mesh=mesh,
        in_specs=(wide, wide, wide, wide, flat, flat),
        out_specs=(wide, wide, wide, wide),
        check_vma=False,
    )
```

```python
import functools
import math

import jax
import jax.numpy as jnp
from jax import lax
from jax.experimental import pallas as pl
from jax.experimental.pallas import tpu as pltpu
from jax.sharding import PartitionSpec as P


HEAD_DIM = 128
WINDOW = 512
MASKED = -1e30
FLOOR = -1e20
META_ROWS = 16
MARKS = 8


bf16, f32 = jnp.bfloat16, jnp.float32
VMEM = pl.BlockSpec(memory_space=pltpu.VMEM)
HBM = pl.BlockSpec(memory_space=pltpu.HBM)
SCALE = 1.0 / math.sqrt(HEAD_DIM)


def dot_nt(a, b):
    return lax.dot_general(a, b, (((1,), (1,)), ((), ())), preferred_element_type=f32)


def dot_nn(a, b):
    return lax.dot_general(a, b, (((1,), (0,)), ((), ())), preferred_element_type=f32)


def route_x(n, cross):
    return [(i, i ^ (3 if cross else 2)) for i in range(n)]


def route_diag(n, cross):
    route = []
    for i in range(n):
        j = i + 2 if (i >> 1) & 1 else i - 2
        route.append((i, j ^ cross if 0 <= j < n else i ^ 1))
    return route


def route_even(n, cross):
    return [(i, i ^ (5 if cross else 4)) for i in range(n)]


def route_odd(n, cross):
    route = []
    for i in range(n):
        j = i + 4 if (i >> 2) & 1 else i - 4
        route.append((i, j ^ cross if 0 <= j < n else i ^ 1))
    return route


class Place:
    def __init__(self, chips):
        index = lax.axis_index("seq")
        self.core = lax.rem(index, 2)
        self.pair = lax.rem(lax.div(index, 2), 2)
        self.odd = lax.rem(lax.div(index, 4), 2)
        self.is_one, self.is_odd = self.pair == 1, self.odd == 1
        chip = lax.div(index, 2)
        self.left_1, self.left_2 = chip >= 1, chip >= 2
        self.right_1, self.right_2 = chip < chips - 1, chip < chips - 2

    def left(self, x, d, a, b):
        return jnp.where(self.is_one, x, d), jnp.where(self.is_odd, a, b)

    def right(self, x, d, a, b):
        return jnp.where(self.is_one, d, x), jnp.where(self.is_odd, b, a)


def tile_of(held, n, group, heads, h):
    start = pl.multiple_of((group * heads + h) * HEAD_DIM, HEAD_DIM)
    return held[n, :, pl.ds(start, HEAD_DIM)]


def fill_halo(heads, rows, held, n, group, pair, odd, refs):
    xs, ds, as_, bs = refs
    for one in (0, 1):
        for two in (0, 1):

            @pl.when((pair == one) & (odd == two))
            def _():
                if n < 2:
                    targets = (ds if one else xs), (bs if two else as_)
                else:
                    targets = (xs if one else ds), (as_ if two else bs)
                for h in range(heads):
                    value = tile_of(held, n, group, heads, h)
                    at = ((n % 2) * heads + h) * rows
                    for ref in targets:
                        ref[at : at + rows, :] = value


def prep_kernel(
    heads, rows, q, k, v, g, doc, loss,
    x1, a1, b1, d1, mine, held, doc_held, loss_held, sems,
):
    copies = []
    targets = (held.at[0], held.at[1], held.at[2], held.at[3], doc_held, loss_held)
    for n, (ref, target) in enumerate(zip((k, v, q, g, doc, loss), targets)):
        copy = pltpu.make_async_copy(ref, target, sems.at[n])
        copy.start()
        copies.append(copy)
    for copy in copies[4:]:
        copy.wait()
    index = lax.axis_index("seq")
    core = lax.rem(index, 2)
    pair = lax.rem(lax.div(index, 2), 2)
    odd = lax.rem(lax.div(index, 4), 2)

    value = (doc_held[...] * 2 + loss_held[...]).astype(f32)
    value = jnp.concatenate([value] * (rows // value.shape[1]), axis=1)
    lane = lax.broadcasted_iota(jnp.int32, (1, rows), 1)
    mine_here = lax.div(lane, doc.shape[1]) == lax.axis_index("head")
    value = jnp.where(mine_here, value, 0.0)
    mine[...] = jnp.broadcast_to(value, (MARKS, rows))
    high = jnp.floor(value * (1.0 / 256.0))
    row = lax.broadcasted_iota(jnp.int32, (META_ROWS, rows), 0)
    low = value - high * 256.0
    meta = jnp.where(row == 0, high, jnp.where(row == 1, low, 0.0)).astype(bf16)
    for ref in (x1, a1, b1, d1):
        ref[2 * heads * rows :, :] = meta
    for n in range(4):
        copies[n].wait()
        fill_halo(heads, rows, held, n, core, pair, odd, (x1, d1, a1, b1))


def rest_kernel(heads, rows, held, x2, a2, b2, d2, cc, oo):
    index = lax.axis_index("seq")
    core = lax.rem(index, 2)
    pair = lax.rem(lax.div(index, 2), 2)
    odd = lax.rem(lax.div(index, 4), 2)
    for n in range(4):
        fill_halo(heads, rows, held, n, 1 - core, pair, odd, (x2, d2, a2, b2))
        for h in range(heads):
            at = (((n + 2) % 4) * heads + h) * rows
            oo[at : at + rows, :] = tile_of(held, n, core, heads, h)
            cc[at : at + rows, :] = tile_of(held, n, 1 - core, heads, h)


def marks_kernel(heads, rows, mine, x1, d1, a1, b1, out):
    line = lax.broadcasted_iota(jnp.int32, (MARKS, rows), 0)
    total = jnp.where(line == 0, mine[...], 0.0)
    at = 2 * heads * rows
    for n, ref in enumerate((x1, d1, a1, b1)):
        meta = ref[at : at + META_ROWS, :].astype(f32)
        total = jnp.where(line == n + 1, meta[0:1, :] * 256.0 + meta[1:2, :], total)
    out[...] = total


def split_marks(one, two):
    value = one[...] + two[...]
    doc = jnp.floor(value * 0.5)
    return doc, value - 2.0 * doc


def side_docs(place, doc, left):
    lines = [doc[n : n + 1, :] for n in range(1, 5)]
    one, two = place.left(*lines) if left else place.right(*lines)
    fine_1, fine_2 = (place.left_1, place.left_2) if left else (place.right_1, place.right_2)
    return [jnp.where(fine_1, one, -1.0), jnp.where(fine_2, two, -1.0)]


def side_loss(place, loss, left):
    lines = [loss[n : n + 1, :] for n in range(1, 5)]
    return list(place.left(*lines) if left else place.right(*lines))


def column_of(row):
    return jnp.transpose(jnp.broadcast_to(row, (HEAD_DIM, row.shape[1])))


def chip_positions(core, rows, axis, shape):
    spot = lax.broadcasted_iota(jnp.int32, shape, axis)
    return spot + jnp.where(spot < rows, core * rows, -core * rows)


def fill_bias(bias, place, rows, own_doc, docs, offsets, sign):
    own = chip_positions(place.core, rows, 0, (2 * rows, HEAD_DIM))
    spot = lax.broadcasted_iota(jnp.int32, (2 * rows, HEAD_DIM), 1)
    for n, (doc, offset) in enumerate(zip(docs, offsets)):
        gap = (own - (spot + offset)) * sign
        fine = (gap >= 0) & (gap < WINDOW) & (own_doc == doc)
        bias[:, n * rows : (n + 1) * rows] = jnp.where(fine, 0.0, MASKED)


def chip_tiles(oo, cc, heads, rows, n, h):
    at = (n * heads + h) * rows
    return [oo[at : at + rows, :], cc[at : at + rows, :]]


def halo_tiles(choose, refs, heads, rows, n, h):
    at = (n * heads + h) * rows
    return list(choose(*(ref[at : at + rows, :] for ref in refs)))


def spread(column):
    return jnp.broadcast_to(column, (column.shape[0], HEAD_DIM))


def widen(value, like):
    return jnp.concatenate([value] * (like.shape[1] // value.shape[1]), axis=1)


def row_max(value):
    return spread(jnp.max(value, axis=1, keepdims=True))


def row_sum(value):
    return spread(jnp.sum(value, axis=1, keepdims=True))


def head_rows(heads, rows):
    return [slice(h * 2 * rows, (h + 1) * 2 * rows) for h in range(heads)]


def stacked(tiles):
    return jnp.concatenate(tiles, axis=0)


def query_own(heads, chips, mark, mark_y, mark_c, mark_b, oo, cc, top_s, norm_s, guess_s, o_s, w_s, u_s, bias):
    place = Place(chips)
    rows = oo.shape[0] // (4 * heads)
    own = [split_marks(mark, mark_y)[0][0:1, :], split_marks(mark_c, mark_b)[0][0:1, :]]
    q_doc = column_of(jnp.concatenate(own, axis=1))
    here, there = place.core * rows, (1 - place.core) * rows
    fill_bias(bias, place, rows, q_doc, own, [here, there], 1)
    span, at = range(heads), head_rows(heads, rows)
    tiles = functools.partial(chip_tiles, oo, cc, heads, rows)
    q_rows, g_rows, k_rows, v_rows = ([stacked(tiles(n, h)) for h in span] for n in range(4))
    score = [dot_nt(q_rows[h], k_rows[h]) * SCALE + bias[...] for h in span]
    top = [row_max(score[h]) for h in span]
    prob = [jnp.exp(score[h] - widen(top[h], score[h])) for h in span]
    norm = [row_sum(prob[h]) for h in span]
    sides = [jnp.concatenate([v_rows[h], k_rows[h]], axis=1) for h in span]
    both = [dot_nn(prob[h].astype(bf16), sides[h]) for h in span]
    grad = [dot_nt(g_rows[h], v_rows[h]) for h in span]
    for h in span:
        out = both[h][:, :HEAD_DIM]
        guess = row_sum(g_rows[h].astype(f32) * out) / norm[h]
        slope = (prob[h] * (grad[h] - widen(guess, grad[h]))).astype(bf16)
        top_s[at[h], :], norm_s[at[h], :], guess_s[at[h], :] = top[h], norm[h], guess
        o_s[at[h], :], w_s[at[h], :] = out, both[h][:, HEAD_DIM:]
        u_s[at[h], :] = dot_nn(slope, k_rows[h])


def query_near(
    heads, chips, mark, mark_y, mark_c, mark_b, oo, cc, x1, d1, a1, b1, top_i, norm_i, guess_i, o_i, w_i, u_i,
    top_s, norm_s, guess_s, o_s, w_s, u_s, weight, bias,
):
    place = Place(chips)
    rows = oo.shape[0] // (4 * heads)
    doc_a, loss_a = split_marks(mark, mark_y)
    doc_b, loss_b = split_marks(mark_c, mark_b)
    own = [doc_a[0:1, :], doc_b[0:1, :]]
    own_loss = [loss_a[0:1, :], loss_b[0:1, :]]
    left_a, left_b = side_docs(place, doc_a, True), side_docs(place, doc_b, True)
    right_a, right_b = side_docs(place, doc_a, False), side_docs(place, doc_b, False)
    q_doc = column_of(jnp.concatenate(own, axis=1))
    q_loss = column_of(jnp.concatenate(own_loss, axis=1))
    losses = own_loss
    for left in (True, False):
        losses = losses + side_loss(place, loss_a, left) + side_loss(place, loss_b, left)
    total = jnp.zeros((2 * rows, HEAD_DIM), f32)
    for doc, loss in zip(own + left_a + left_b + right_a + right_b, losses):
        total = total + jnp.where(q_doc == doc, loss, 0.0)
    weight[...] = q_loss * (float(rows) / jnp.maximum(row_sum(total), float(rows // 8)))

    here = place.core * rows
    fill_bias(bias, place, rows, q_doc, left_a, [here - 2 * rows, here - 4 * rows], 1)
    span, at = range(heads), head_rows(heads, rows)
    tiles = functools.partial(chip_tiles, oo, cc, heads, rows)
    halo = functools.partial(halo_tiles, place.left, (x1, d1, a1, b1), heads, rows)
    q_rows, g_rows = ([stacked(tiles(n, h)) for h in span] for n in range(2))
    k_rows, v_rows = ([stacked(halo(n, h)) for h in span] for n in range(2))
    score = [dot_nt(q_rows[h], k_rows[h]) * SCALE + bias[...] for h in span]
    top = [jnp.maximum(row_max(score[h]), top_i[at[h], :]) for h in span]
    prob = [jnp.exp(score[h] - widen(top[h], score[h])) for h in span]
    fade = [jnp.exp(top_i[at[h], :] - top[h]) for h in span]
    norm = [norm_i[at[h], :] * fade[h] + row_sum(prob[h]) for h in span]
    sides = [jnp.concatenate([v_rows[h], k_rows[h]], axis=1) for h in span]
    both = [dot_nn(prob[h].astype(bf16), sides[h]) for h in span]
    grad = [dot_nt(g_rows[h], v_rows[h]) for h in span]
    for h in span:
        out = o_i[at[h], :] * fade[h] + both[h][:, :HEAD_DIM]
        guess = row_sum(g_rows[h].astype(f32) * out) / norm[h]
        slope = (prob[h] * (grad[h] - widen(guess, grad[h]))).astype(bf16)
        older = w_i[at[h], :]
        based = (u_i[at[h], :] - older * (guess - guess_i[at[h], :])) * fade[h]
        top_s[at[h], :], norm_s[at[h], :], guess_s[at[h], :] = top[h], norm[h], guess
        o_s[at[h], :], w_s[at[h], :] = out, older * fade[h] + both[h][:, HEAD_DIM:]
        u_s[at[h], :] = based + dot_nn(slope, k_rows[h])


def query_late(
    heads, chips, mark, mark_y, mark_c, mark_b, oo, cc, x2, d2, a2, b2, top_i, norm_i, guess_i, o_i, weight,
    att_own, att_other, stats, prob_l, fade_l, delta_l, gap_l, coef_l, bias,
):
    place = Place(chips)
    rows = oo.shape[0] // (4 * heads)
    doc_a, _ = split_marks(mark, mark_y)
    doc_b, _ = split_marks(mark_c, mark_b)
    q_doc = column_of(jnp.concatenate([doc_a[0:1, :], doc_b[0:1, :]], axis=1))
    there = (1 - place.core) * rows
    offsets = [there - 2 * rows, there - 4 * rows]
    fill_bias(bias, place, rows, q_doc, side_docs(place, doc_b, True), offsets, 1)
    span, at = range(heads), head_rows(heads, rows)
    tiles = functools.partial(chip_tiles, oo, cc, heads, rows)
    halo = functools.partial(halo_tiles, place.left, (x2, d2, a2, b2), heads, rows)
    q_rows = [stacked(tiles(0, h)) for h in span]
    k_rows, v_rows = ([stacked(halo(n, h)) for h in span] for n in range(2))
    score = [dot_nt(q_rows[h], k_rows[h]) * SCALE + bias[...] for h in span]
    top = [jnp.maximum(row_max(score[h]), top_i[at[h], :]) for h in span]
    prob = [jnp.exp(score[h] - widen(top[h], score[h])) for h in span]
    fade = [jnp.exp(top_i[at[h], :] - top[h]) for h in span]
    norm = [norm_i[at[h], :] * fade[h] + row_sum(prob[h]) for h in span]
    half = [prob[h].astype(bf16) for h in span]
    mixed = [dot_nn(half[h], v_rows[h]) for h in span]
    share = [1.0 / norm[h] for h in span]
    att = [((o_i[at[h], :] * fade[h] + mixed[h]) * share[h]).astype(bf16) for h in span]
    g_rows = [stacked(tiles(1, h)).astype(f32) for h in span]
    delta = [row_sum(g_rows[h] * att[h].astype(f32)) for h in span]
    lane = lax.broadcasted_iota(jnp.int32, (2 * rows, HEAD_DIM), 1)
    scale = weight[...]
    out = jnp.where(lane == 2 * heads, scale, 0.0)
    for h in span:
        out = jnp.where(lane == h, top[h] + jnp.log(norm[h]), out)
        out = jnp.where(lane == heads + h, delta[h], out)
        prob_l[at[h], :] = half[h]
        att_own[h * rows : (h + 1) * rows, :] = att[h][:rows]
        att_other[h * rows : (h + 1) * rows, :] = att[h][rows:]
        fade_l[at[h], :], delta_l[at[h], :] = fade[h], delta[h]
        gap_l[at[h], :] = delta[h] - guess_i[at[h], :]
        coef_l[at[h], :] = share[h] * scale * SCALE
    stats[...] = jnp.transpose(out)[:META_ROWS, :]


def key_part(heads, rows, k_rows, v_rows, q_rows, g_rows, bias, prob_out, slope_out, known_out):
    span, at = range(heads), head_rows(heads, rows)
    score = [dot_nt(k_rows[h], q_rows[h]) * SCALE + bias[...] for h in span]
    top = [jnp.maximum(jnp.max(score[h], axis=0, keepdims=True), FLOOR) for h in span]
    prob = [jnp.exp(score[h] - top[h]) for h in span]
    grad = [dot_nt(v_rows[h], g_rows[h]) for h in span]
    for h in span:
        norm = jnp.maximum(jnp.sum(prob[h], axis=0, keepdims=True), 1.0)
        guess = jnp.sum(prob[h] * grad[h], axis=0, keepdims=True) / norm
        prob_out[at[h], :] = prob[h].astype(bf16)
        slope_out[at[h], :] = (prob[h] * (grad[h] - guess)).astype(bf16)
        known_out[h : h + 1, :] = top[h]
        known_out[heads + h : heads + h + 1, :] = guess


def key_own(heads, chips, mark, mark_y, mark_c, mark_b, oo, cc, prob_out, slope_out, known_out, bias):
    place = Place(chips)
    rows = oo.shape[0] // (4 * heads)
    own = [split_marks(mark, mark_y)[0][0:1, :], split_marks(mark_c, mark_b)[0][0:1, :]]
    k_doc = column_of(jnp.concatenate(own, axis=1))
    here, there = place.core * rows, (1 - place.core) * rows
    fill_bias(bias, place, rows, k_doc, own, [here, there], -1)
    tiles = functools.partial(chip_tiles, oo, cc, heads, rows)
    q_rows, g_rows, k_rows, v_rows = (
        [stacked(tiles(n, h)) for h in range(heads)] for n in range(4)
    )
    key_part(heads, rows, k_rows, v_rows, q_rows, g_rows, bias, prob_out, slope_out, known_out)


def key_halo(heads, place, rows, mark, mark_y, mark_c, mark_b, oo, cc, refs, near, outs, bias):
    doc_a, _ = split_marks(mark, mark_y)
    doc_b, _ = split_marks(mark_c, mark_b)
    k_doc = column_of(jnp.concatenate([doc_a[0:1, :], doc_b[0:1, :]], axis=1))
    first = (place.core if near else 1 - place.core) * rows
    docs = side_docs(place, doc_a if near else doc_b, False)
    fill_bias(bias, place, rows, k_doc, docs, [first + 2 * rows, first + 4 * rows], -1)
    tiles = functools.partial(chip_tiles, oo, cc, heads, rows)
    halo = functools.partial(halo_tiles, place.right, refs, heads, rows)
    k_rows, v_rows = ([stacked(tiles(n, h)) for h in range(heads)] for n in (2, 3))
    q_rows, g_rows = ([stacked(halo(n, h)) for h in range(heads)] for n in range(2))
    key_part(heads, rows, k_rows, v_rows, q_rows, g_rows, bias, *outs)


def key_near(
    heads, chips, mark, mark_y, mark_c, mark_b, oo, cc, x1, d1, a1, b1, prob_out, slope_out, known_out, bias
):
    place = Place(chips)
    rows = oo.shape[0] // (4 * heads)
    outs = (prob_out, slope_out, known_out)
    key_halo(heads, place, rows, mark, mark_y, mark_c, mark_b, oo, cc, (x1, d1, a1, b1), True, outs, bias)


def both_late(
    heads, chips, mark, mark_y, mark_c, mark_b, oo, cc, x2, d2, a2, b2, u_i, w_i,
    prob_l, fade_l, delta_l, gap_l, coef_l, att_other,
    dq_own, send, prob_out, slope_out, known_out, bias,
):
    place = Place(chips)
    rows = oo.shape[0] // (4 * heads)
    refs = (x2, d2, a2, b2)
    tiles = functools.partial(chip_tiles, oo, cc, heads, rows)
    halo = functools.partial(halo_tiles, place.left, refs, heads, rows)
    span, at = range(heads), head_rows(heads, rows)
    g_rows = [stacked(tiles(1, h)) for h in span]
    k_rows, v_rows = ([stacked(halo(n, h)) for h in span] for n in range(2))
    grad = [dot_nt(g_rows[h], v_rows[h]) for h in span]
    grad = [grad[h] - widen(delta_l[at[h], :], grad[h]) for h in span]
    slope = [(prob_l[at[h], :].astype(f32) * grad[h]).astype(bf16) for h in span]
    part = [dot_nn(slope[h], k_rows[h]) for h in span]
    for h in span:
        early = (u_i[at[h], :] - w_i[at[h], :] * gap_l[at[h], :]) * fade_l[at[h], :]
        dq = ((early + part[h]) * coef_l[at[h], :]).astype(bf16)
        dq_own[h * rows : (h + 1) * rows, :] = dq[:rows]
        send[(heads + h) * rows : (heads + h + 1) * rows, :] = dq[rows:]
    send[: heads * rows, :] = att_other[...]
    outs = (prob_out, slope_out, known_out)
    key_halo(heads, place, rows, mark, mark_y, mark_c, mark_b, oo, cc, refs, False, outs, bias)


def key_final(
    heads, chips, oo, cc, x1, d1, a1, b1, x2, d2, a2, b2,
    prob_o, slope_o, known_o, prob_e, slope_e, known_e, prob_l, slope_l, known_l,
    stats, stats_1, stats_a, stats_b, dk_own, dv_own, send,
):
    place = Place(chips)
    rows = oo.shape[0] // (4 * heads)
    own, one = stats[...], stats_1[...]
    two = jnp.where(place.is_odd, stats_b[...], stats_a[...])
    parts = [own, one[:, :rows], two[:, :rows], one[:, rows:], two[:, rows:]]
    line = jnp.concatenate(parts, axis=1)
    known = jnp.concatenate([known_o[...], known_e[...], known_l[...]], axis=1)
    scale = jnp.exp(known[:heads] - line[:heads]) * line[2 * heads : 2 * heads + 1]
    gap = known[heads : 2 * heads] - line[heads : 2 * heads]
    near, far = (x1, d1, a1, b1), (x2, d2, a2, b2)
    span, at = range(heads), head_rows(heads, rows)

    def tiles(n, h):
        return stacked(
            chip_tiles(oo, cc, heads, rows, n, h)
            + halo_tiles(place.right, near, heads, rows, n, h)
            + halo_tiles(place.right, far, heads, rows, n, h)
        )

    for h in span:
        prob = jnp.concatenate([prob_o[at[h], :], prob_e[at[h], :], prob_l[at[h], :]], axis=1)
        slope = jnp.concatenate([slope_o[at[h], :], slope_e[at[h], :], slope_l[at[h], :]], axis=1)
        scale_h = scale[h : h + 1, :].astype(bf16)
        slope = (slope + prob * gap[h : h + 1, :].astype(bf16)) * scale_h
        dv = dot_nn(prob * scale_h, tiles(1, h)).astype(bf16)
        dk = (dot_nn(slope, tiles(0, h)) * SCALE).astype(bf16)
        dk_own[h * rows : (h + 1) * rows, :] = dk[:rows]
        dv_own[h * rows : (h + 1) * rows, :] = dv[:rows]
        send[h * rows : (h + 1) * rows, :] = dk[rows:]
        send[(heads + h) * rows : (heads + h + 1) * rows, :] = dv[rows:]


def put_halves(heads, rows, part, skip, out, group, sems, copies):
    for h in range(heads):
        start = pl.multiple_of((group * heads + h) * HEAD_DIM, HEAD_DIM)
        copy = pltpu.make_async_copy(
            part.at[pl.ds((skip + h) * rows, rows)],
            out.at[:, pl.ds(start, HEAD_DIM)],
            sems.at[len(copies)],
        )
        copy.start()
        copies.append(copy)


def join_first(heads, one, two, got, three, four, out_1, out_2, out_3, out_4, sems):
    core = lax.rem(lax.axis_index("seq"), 2)
    rows = out_1.shape[0]
    copies = []
    for part, out in ((one, out_1), (two, out_2), (three, out_3), (four, out_4)):
        put_halves(heads, rows, part, 0, out, core, sems, copies)
    put_halves(heads, rows, got, 0, out_1, 1 - core, sems, copies)
    put_halves(heads, rows, got, heads, out_2, 1 - core, sems, copies)
    for copy in copies:
        copy.wait()


def join_last(heads, begun_1, begun_2, got, out_1, out_2, sems):
    core = lax.rem(lax.axis_index("seq"), 2)
    rows = out_1.shape[0]
    copies = []
    put_halves(heads, rows, got, 0, out_1, 1 - core, sems, copies)
    put_halves(heads, rows, got, heads, out_2, 1 - core, sems, copies)
    for copy in copies:
        copy.wait()


def run(kernel, outs, args, scratch=(), flops=0, hbm_in=0, hbm_out=False, alias=None):
    size = sum(math.prod(a.shape) * a.dtype.itemsize for a in args)
    size = size + sum(math.prod(o.shape) * o.dtype.itemsize for o in outs)
    far = [pltpu.with_memory_space_constraint(a, pltpu.HBM) for a in args[:hbm_in]]
    kept = [pltpu.with_memory_space_constraint(a, pltpu.VMEM) for a in args[hbm_in:]]
    return pl.pallas_call(
        kernel,
        out_shape=[o if hbm_out else pltpu.VMEM(o.shape, o.dtype) for o in outs],
        in_specs=[HBM] * hbm_in + [VMEM] * len(kept),
        out_specs=[HBM if hbm_out else VMEM] * len(outs),
        scratch_shapes=list(scratch),
        input_output_aliases=alias or {},
        compiler_params=pltpu.CompilerParams(vmem_limit_bytes=24 << 20),
        cost_estimate=pl.CostEstimate(flops=flops, bytes_accessed=size, transcendentals=0),
    )(*far, *kept)


def body(queries, keys, values, grad_out, doc_ids, loss_mask):
    rows, width = queries.shape
    heads = width // HEAD_DIM // 2
    n = lax.axis_size("seq")
    chips = n // 2
    shape = jax.ShapeDtypeStruct

    def move(value, route, axis="seq"):
        return lax.ppermute(value, axis, route)

    core_swap = [(i, i ^ 1) for i in range(n)]
    piece = 2 * heads * rows
    marked = shape((piece + META_ROWS, HEAD_DIM), bf16)
    plain = shape((piece, HEAD_DIM), bf16)
    double = shape((2 * piece, HEAD_DIM), bf16)
    marks = shape((MARKS, rows), f32)
    x1, a1, b1, d1, mine, held = run(
        functools.partial(prep_kernel, heads, rows),
        [marked] * 4 + [marks, shape((4, rows, width), bf16)],
        (queries, keys, values, grad_out, doc_ids[None, :], loss_mask[None, :]),
        [
            pltpu.VMEM((1, doc_ids.shape[0]), doc_ids.dtype),
            pltpu.VMEM((1, loss_mask.shape[0]), loss_mask.dtype),
            pltpu.SemaphoreType.DMA((6,)),
        ],
        hbm_in=6,
    )
    x2, a2, b2, d2, cc, oo = run(
        functools.partial(rest_kernel, heads, rows), [plain] * 4 + [double, double], (held,)
    )
    x1 = move(x1, route_x(n, 0))
    a1 = move(a1, route_even(n, 0))
    b1 = move(b1, route_odd(n, 0))
    d1 = move(d1, route_diag(n, 0))
    x2 = move(x2, route_x(n, 1))
    a2 = move(a2, route_even(n, 1))
    b2 = move(b2, route_odd(n, 1))
    d2 = move(d2, route_diag(n, 1))
    cc = move(cc, core_swap)

    head_swap = [(0, 1), (1, 0)]
    both_swap = [(2 * i + k, 2 * (i ^ 1) + 1 - k) for i in range(n) for k in range(2)]

    def complete(part):
        over_y = move(part, head_swap, "head")
        over_core = move(part, core_swap)
        over_both = move(part, both_swap, ("seq", "head"))
        return part, over_y, over_core, over_both

    own_marks = complete(mine)
    halves = run(functools.partial(marks_kernel, heads, rows), [marks], (mine, x1, d1, a1, b1))[0]
    all_marks = complete(halves)

    near, far = (x1, d1, a1, b1), (x2, d2, a2, b2)
    tall = shape((heads * 2 * rows, HEAD_DIM), f32)
    table = shape((2 * rows, HEAD_DIM), f32)
    rest = shape((META_ROWS, 2 * rows), f32)
    part = shape((heads * rows, HEAD_DIM), bf16)
    square = shape((heads * 2 * rows, 2 * rows), bf16)
    known = shape((MARKS, 2 * rows), f32)
    bias = [pltpu.VMEM((2 * rows, 2 * rows), f32)]
    block = 2 * heads * (2 * rows) * (2 * rows) * HEAD_DIM

    def work(kernel, outs, args, amount, scratch=bias):
        kernel = functools.partial(kernel, heads, chips)
        return run(kernel, outs, args, scratch, amount * block)

    own_args = own_marks + (oo, cc)
    all_args = all_marks + (oo, cc)
    state = work(query_own, [tall] * 6, own_args, 5)
    prob_o, slope_o, known_o = work(key_own, [square, square, known], own_args, 2)
    *state, weight = work(query_near, [tall] * 6 + [table], all_args + near + tuple(state), 5)
    prob_e, slope_e, known_e = work(key_near, [square, square, known], all_args + near, 2)
    top_s, norm_s, guess_s, o_s, w_s, u_s = state
    att_own, att_other, stats, *kept = work(
        query_late,
        [part, part, rest, square] + [tall] * 4,
        all_args + far + (top_s, norm_s, guess_s, o_s, weight),
        2,
    )
    stats_1 = move(stats, [(i, (i - 2) % n) for i in range(n)])
    stats_a = move(stats, route_even(n, 0))
    stats_b = move(stats, route_odd(n, 0))
    dq_own, send_1, prob_l, slope_l, known_l = work(
        both_late,
        [part, plain, square, square, known],
        all_args + far + (u_s, w_s) + tuple(kept) + (att_other,),
        4,
    )
    got_1 = move(send_1, core_swap)
    dk_own, dv_own, send_2 = work(
        key_final,
        [part, part, plain],
        (oo, cc)
        + near
        + far
        + (prob_o, slope_o, known_o, prob_e, slope_e, known_e, prob_l, slope_l, known_l)
        + (stats, stats_1, stats_a, stats_b),
        6,
        (),
    )
    got_2 = move(send_2, core_swap)
    whole = shape((rows, width), bf16)
    sems = [pltpu.SemaphoreType.DMA((6 * heads,))]
    attended, query_grad, key_grad, value_grad = run(
        functools.partial(join_first, heads),
        [whole] * 4,
        (att_own, dq_own, got_1, dk_own, dv_own),
        sems,
        hbm_out=True,
    )
    key_grad, value_grad = run(
        functools.partial(join_last, heads),
        [whole, whole],
        (key_grad, value_grad, got_2),
        sems,
        hbm_in=2,
        hbm_out=True,
        alias={0: 0, 1: 1},
    )
    return attended, query_grad, key_grad, value_grad


def solution(mesh):
    wide = P("seq", "head")
    flat = P(("seq", "head"))
    return jax.shard_map(
        body,
        mesh=mesh,
        in_specs=(wide, wide, wide, wide, flat, flat),
        out_specs=(wide, wide, wide, wide),
        check_vma=False,
    )
```
